32 devices in a mesh: section: 2 (over x), expert: 4 (over z), shard: 4 (over y, core).
Axes of the slice: x: 2, y: 2, z: 4, core: 2. Of those that a mesh axis runs over, the one named last changes fastest.
Arguments:
- fwd_in: bfloat16 [2, 512, 3584], P('section', 'expert', 'shard'), may hold values from -6 to 6
- saved_in: bfloat16 [2, 512, 3584], P('section', 'expert', 'shard'), may hold values from -6 to 6
- grad_in: bfloat16 [2, 512, 3584], P('section', 'expert', 'shard'), may hold values from -6 to 6
- w_in: bfloat16 [2, 4, 3584, 1024], P('section', 'expert', 'shard'), may hold values from -0.09375 to 0.09375
- w_out: bfloat16 [2, 4, 1024, 3584], P('section', 'expert', None, 'shard'), may hold values from -0.1875 to 0.1875
- ids_fwd: int32 [2, 512, 2], P('section', 'expert'), may hold values from 0 to 3, all different within a row; in each aligned block of 128 rows (0 to 127, 128 to 255, ..., all dimensions but the last counted through in order) at most 80 rows name the same one
- weight_fwd: int32 [2, 512, 2], P('section', 'expert'), may hold values from 3277 to 65535
- ids_bwd: int32 [2, 512, 2], P('section', 'expert'), may hold values from 0 to 3, all different within a row; in each aligned block of 128 rows (0 to 127, 128 to 255, ..., all dimensions but the last counted through in order) at most 80 rows name the same one
- weight_bwd: int32 [2, 512, 2], P('section', 'expert'), may hold values from 3277 to 65535
Outputs:
- fwd_out: bfloat16 [2, 512, 3584], P('section', 'expert', 'shard')
- bwd_out: bfloat16 [2, 512, 3584], P('section', 'expert', 'shard')
The draws below stay inside these ranges and needn't reach their ends.
Inputs may be any that keep to these rules, and one draw needn't show every extreme that they name: `ids_fwd`: the 2 experts of a token differ. In each layer, among the 128 tokens of one index of the expert axis, no expert is chosen by more than 80 slots. `ids_bwd`: the 2 experts of a token differ. In each layer, among the 128 tokens of one index of the expert axis, no expert is chosen by more than 80 slots.
All inputs are finite; a program needn't handle non-finite values.
Results may differ from the reference program's by a relative error of at most 0.0049.
Values may be sent and summed in bfloat16 or wider, within the bound.
A program may use at most 64 MiB of HBM per device.

```python
import math
import jax
import jax.numpy as jnp
import numpy as np
from jax import lax

D = 3584
FF = 1024
TOP = 2
TOK_E = 128
EXPERTS = 4
TOKENS = 512
LAYERS = 2
CAP = 80


def plant(result, stream_key, smallest, top_value):
    longest = result.shape.index(max(result.shape))
    spots = []
    for shift in (0, 1):
        where = [jax.random.randint(jax.random.fold_in(stream_key, axis), (), 0, length) for axis, length in enumerate(result.shape)]
        where[longest] = (where[longest] + shift) % result.shape[longest]
        spots.append(tuple(where))
    return result.at[spots[0]].set(smallest).at[spots[1]].set(top_value)


def steps_of(rng, extent, pieces, smallest, high):
    factor_of = 1.0
    for dim, parts in pieces:
        draws = jax.random.uniform(jax.random.fold_in(jax.random.fold_in(rng, 6), dim), (parts,), jnp.float32, smallest / len(pieces), high / len(pieces))
        factor_of = factor_of * jnp.repeat(jnp.exp(draws), extent[dim] // parts).reshape((-1,) + (1,) * (len(extent) - 1 - dim))
    return factor_of


def assign_block(key, own, number, rows, number_of, top, reach, skew):
    sequence = jax.random.permutation(key, number_of)
    crowded, usual = portions_of(number_of, rows * top, reach, skew, True), portions_of(number_of, rows * top, reach, skew, False)
    places = jnp.arange(number_of)

    def named(sizes, offset_by):
        used = int((sizes > 0).sum())
        fixed = max(1, used // 4)
        shifted = fixed + (places - fixed + offset_by * (used - fixed)) % max(1, number_of - fixed)
        return jnp.zeros((number_of,), jnp.int32).at[sequence[jnp.where(places < fixed, places, shifted)]].set(jnp.asarray(sizes, jnp.int32))

    sizes = jnp.where(number % 4 == 0, named(crowded, number // 4), named(usual, number - number // 4 - 1))
    mixed = jax.random.permutation(jax.random.fold_in(own, 3), number_of)
    donor, sink = mixed[0:number_of // 2 * 2:2], mixed[1:number_of // 2 * 2:2]
    room = jnp.minimum(sizes[donor] - 1, reach - sizes[sink]) // 2
    room = jnp.where((donor == sequence[0]) | (sink == sequence[0]) | (sizes[sink] == 0), 0, jnp.maximum(room, 0))
    shifted = jax.random.randint(jax.random.fold_in(own, 4), (number_of // 2,), 0, 1 << 20) % (room + 1)
    sizes = sizes.at[donor].add(-shifted).at[sink].add(shifted)
    items = jnp.searchsorted(jnp.cumsum(sizes), jnp.arange(rows * top), side="right").astype(jnp.int32)
    table = items.reshape(top, rows).T
    table = table[jax.random.permutation(jax.random.fold_in(own, 1), rows)]
    offset_by = jax.random.randint(jax.random.fold_in(own, 2), (rows, 1), 0, top)
    return jnp.take_along_axis(table, (jnp.arange(top)[None, :] + offset_by) % top, axis=1)


def portions_of(amount, total, most, lean, full):
    portions = [(1 << 20) // math.isqrt(standing ** lean) + 1 for standing in range(1, amount + 1)]
    largest = most if full else min(most, max(-(-total // amount), total * portions[0] // sum(portions)))
    least = 1 if total - largest >= amount - 1 else 0
    given, rest = [largest] + [least] * (amount - 1), total - largest - least * (amount - 1)
    while rest > 0:
        candidates = [i for i in range(1, amount) if given[i] < largest] or [i for i in range(1, amount) if given[i] < most]
        pool, left = sum([portions[i] for i in candidates]), rest
        for i in candidates:
            addition = min(most - given[i], max(1, left * portions[i] // pool), rest)
            given[i] = given[i] + addition
            rest = rest - addition
    return np.array(given)


def normal_values(stream_key, shape, width, limit, split=(), held_as=jnp.bfloat16):
    factor_of = steps_of(stream_key, shape, split, -0.22, 0.18) if split else 1.0
    drawn = jax.random.normal(stream_key, shape, jnp.float32) * width * factor_of
    return jnp.minimum(jnp.maximum(drawn, -limit), limit).astype(held_as)


def setup_inputs(seed: int = 0) -> dict:
    key_list = jax.random.split(jax.random.key(seed), 10)
    fwd_in = normal_values(key_list[0], (LAYERS, TOKENS, D), 1.0, 6.0, ((0, 2), (1, 4), (2, 4)))
    saved_in = normal_values(key_list[1], (LAYERS, TOKENS, D), 1.0, 6.0, ((0, 2), (1, 4), (2, 4)))
    grad_in = normal_values(key_list[2], (LAYERS, TOKENS, D), 1.0, 6.0, ((0, 2), (1, 4), (2, 4)))
    w_in = normal_values(key_list[3], (LAYERS, EXPERTS, D, FF), D ** -0.5, 0.09375, ((0, 2), (1, 4), (2, 4)))
    w_out = normal_values(key_list[4], (LAYERS, EXPERTS, FF, D), FF ** -0.5, 0.1875, ((0, 2), (1, 4), (3, 4)))
    ids_fwd_keys = jax.random.split(jax.random.fold_in(key_list[5], 1), LAYERS * TOKENS // TOK_E)
    ids_fwd_turns = jax.random.permutation(jax.random.fold_in(key_list[5], 3), LAYERS * TOKENS // TOK_E)
    ids_fwd = jax.vmap(lambda own, number: assign_block(jax.random.fold_in(key_list[5], 2), own, number, TOK_E, EXPERTS, TOP, CAP, 1))(ids_fwd_keys, ids_fwd_turns).reshape((LAYERS, TOKENS, TOP))
    weight_fwd = plant(jax.random.randint(key_list[6], (LAYERS, TOKENS, TOP), 3277, 65536), jax.random.fold_in(key_list[6], 1), 3277, 65535).astype(jnp.int32)
    ids_bwd_keys = jax.random.split(jax.random.fold_in(key_list[7], 1), LAYERS * TOKENS // TOK_E)
    ids_bwd_turns = jax.random.permutation(jax.random.fold_in(key_list[7], 3), LAYERS * TOKENS // TOK_E)
    ids_bwd = jax.vmap(lambda own, number: assign_block(jax.random.fold_in(key_list[7], 2), own, number, TOK_E, EXPERTS, TOP, CAP, 1))(ids_bwd_keys, ids_bwd_turns).reshape((LAYERS, TOKENS, TOP))
    weight_bwd = plant(jax.random.randint(key_list[8], (LAYERS, TOKENS, TOP), 3277, 65536), jax.random.fold_in(key_list[8], 1), 3277, 65535).astype(jnp.int32)
    return dict(fwd_in=fwd_in, saved_in=saved_in, grad_in=grad_in, w_in=w_in, w_out=w_out, ids_fwd=ids_fwd, weight_fwd=weight_fwd, ids_bwd=ids_bwd, weight_bwd=weight_bwd)


def destinations(route_ids, experts, capacity):
    tokens, slot_count = route_ids.shape
    flat_ids = route_ids.reshape(-1)
    labels = jnp.arange(experts, dtype=jnp.int32)
    onehot = (flat_ids[:, None] == labels[None, :]).astype(jnp.int32)
    before = jnp.cumsum(onehot, axis=0) - onehot
    ranking = jnp.sum(before * onehot, axis=1).astype(jnp.int32)
    return (flat_ids * capacity + ranking).reshape(tokens, slot_count).astype(jnp.int32)


def buffer_index(route_ids):
    block_count = route_ids.shape[0] // TOK_E
    grouped = route_ids.reshape(block_count, TOK_E, TOP)

    def one_block(block_ids):
        return destinations(block_ids, EXPERTS, CAP)

    inside = jax.vmap(one_block)(grouped)
    position = inside - grouped * CAP
    block_rows = jnp.arange(block_count, dtype=jnp.int32)[:, None, None]
    slot_index = grouped * (block_count * CAP) + block_rows * CAP + position
    return slot_index.reshape(route_ids.shape).astype(jnp.int32), block_count * CAP


def fill_slots(tok_rows, slot_index, per_expert):
    features = tok_rows.shape[1]
    stacked = jnp.repeat(tok_rows, TOP, axis=0)
    zero_rows = jnp.zeros((EXPERTS * per_expert, features), tok_rows.dtype)
    return zero_rows.at[slot_index.reshape(-1)].set(stacked).reshape(EXPERTS, per_expert, features)


def mix_back(tok_rows, results, slot_index, route_weight):
    picked = results.reshape(EXPERTS * results.shape[1], -1)[slot_index].astype(jnp.float32)
    slot_weight = route_weight.astype(jnp.float32) / 32768.0
    mixed = tok_rows.astype(jnp.float32) + jnp.sum(slot_weight[:, :, None] * picked, axis=1)
    return mixed.astype(jnp.bfloat16)


def forward_layer(layer_args):
    tok_rows, route_ids, route_weight, up_matrix, down_matrix = layer_args
    slot_index, per_expert = buffer_index(route_ids)
    slot_rows = fill_slots(tok_rows, slot_index, per_expert)

    def expert_pass(expert_args):
        rows_here, up_here, down_here = expert_args
        hidden = jnp.dot(rows_here, up_here, preferred_element_type=jnp.float32)
        active = jax.nn.silu(hidden).astype(jnp.bfloat16)
        return jnp.dot(active, down_here, preferred_element_type=jnp.float32).astype(jnp.bfloat16)

    results = lax.map(expert_pass, (slot_rows, up_matrix, down_matrix))
    return mix_back(tok_rows, results, slot_index, route_weight)


def backward_layer(layer_args):
    tok_rows, tok_grads, route_ids, route_weight, up_matrix, down_matrix = layer_args
    slot_index, per_expert = buffer_index(route_ids)
    slot_rows = fill_slots(tok_rows, slot_index, per_expert)
    slot_grads = fill_slots(tok_grads, slot_index, per_expert)

    def expert_pass(expert_args):
        rows_here, grads_here, up_here, down_here = expert_args
        hidden = jnp.dot(rows_here, up_here, preferred_element_type=jnp.float32)
        slope_in = jnp.dot(grads_here, down_here.T, preferred_element_type=jnp.float32)
        squash = jax.nn.sigmoid(hidden)
        slope = (slope_in * squash * (1.0 + hidden * (1.0 - squash))).astype(jnp.bfloat16)
        return jnp.dot(slope, up_here.T, preferred_element_type=jnp.float32).astype(jnp.bfloat16)

    results = lax.map(expert_pass, (slot_rows, slot_grads, up_matrix, down_matrix))
    return mix_back(tok_grads, results, slot_index, route_weight)


def reference(fwd_in, saved_in, grad_in, w_in, w_out, ids_fwd, weight_fwd, ids_bwd, weight_bwd):
    layer_outs = lax.map(forward_layer, (fwd_in, ids_fwd, weight_fwd, w_in, w_out))
    layer_grads = lax.map(backward_layer, (saved_in, grad_in, ids_bwd, weight_bwd, w_in, w_out))
    fwd_out = jnp.roll(layer_outs, 1, axis=0)
    bwd_out = jnp.roll(layer_grads, -1, axis=0)
    return fwd_out, bwd_out
```

```python
import functools

import jax
import jax.numpy as jnp
from jax import lax
from jax.experimental import pallas as pl
from jax.experimental.pallas import tpu as pltpu
from jax.sharding import PartitionSpec as P

MESH = pl.DeviceIdType.MESH
LANES = 128
ROWS = 16


def column_chunks(features):
    chunks, start = [], 0
    while start < features:
        size = min(3 * LANES, features - start)
        chunks.append((start, size))
        start += size
    return chunks


def kernel(dims, meta, fwd_in, saved_in, grad_in, w_in_hbm, w_out_hbm, fwd_out, bwd_out,
           w_in, w_out, pick, mix_hi, mix_lo, packed, slots, part_out, part_in, act,
           ret_out, ret_in, done, w_sem, disp_s, disp_r, part_s, part_r, act_s, act_r,
           ret_s, ret_r, hop_s, hop_r):
    sections, group, shards, cap, tokens, features, quarter, groups = dims
    per_group = group // groups
    span = per_group * cap
    chunks = column_chunks(features)
    sec = lax.axis_index("section")
    me = lax.axis_index("expert")
    mine = lax.axis_index("shard")

    load_in = pltpu.make_async_copy(w_in_hbm.at[0, 0], w_in, w_sem.at[0])
    load_out = pltpu.make_async_copy(w_out_hbm.at[0, 0], w_out, w_sem.at[1])
    load_in.start()
    load_out.start()

    def expert_peer(k):
        return (sec, lax.rem(me + k, group), mine)

    def shard_peer(k):
        return (sec, me, lax.rem(mine + k, shards))

    def section_peer(k):
        return (lax.rem(sec + k + sections, sections), me, mine)

    barrier = pltpu.get_barrier_semaphore()
    peers = [expert_peer(k) for k in range(1, group)]
    peers += [shard_peer(k) for k in range(1, shards)]
    peers += [section_peer(1), section_peer(-1)]
    for peer in peers:
        pl.semaphore_signal(barrier, inc=1, device_id=peer, device_id_type=MESH)

    upper = (lax.broadcasted_iota(jnp.int32, (tokens, tokens), 0)
             < lax.broadcasted_iota(jnp.int32, (tokens, tokens), 1)).astype(jnp.bfloat16)
    height = max(group, 8)
    labels = lax.rem(lax.broadcasted_iota(jnp.int32, (height, tokens), 0) + me, group)
    spots = lax.broadcasted_iota(jnp.int32, (cap, tokens), 0)
    for way in range(2):
        base = 4 * way
        first = jnp.broadcast_to(meta[base : base + 1, :], (height, tokens)) == labels
        second = jnp.broadcast_to(meta[base + 1 : base + 2, :], (height, tokens)) == labels
        q_first = jnp.broadcast_to(meta[base + 2 : base + 3, :], (height, tokens))
        q_second = jnp.broadcast_to(meta[base + 3 : base + 4, :], (height, tokens))
        weight = jnp.where(first, q_first, 0) + jnp.where(second, q_second, 0)
        named = jnp.where(first, 1, 0) + jnp.where(second, 1, 0)
        rank = jnp.dot(named.astype(jnp.float32).astype(jnp.bfloat16), upper,
                       preferred_element_type=jnp.float32).astype(jnp.int32)
        spot = jnp.where(named > 0, rank, cap)
        high = weight >> 8
        low = weight & 255
        for k in range(group):
            hit = jnp.broadcast_to(spot[k : k + 1, :], (cap, tokens)) == spots
            rows = pl.ds(k * cap, cap)
            pick[way, rows, :] = jnp.where(hit, 1.0, 0.0).astype(jnp.bfloat16)
            mix_hi[way, rows, :] = jnp.where(
                hit, jnp.broadcast_to(high[k : k + 1, :], (cap, tokens)), 0
            ).astype(jnp.float32).astype(jnp.bfloat16)
            mix_lo[way, rows, :] = jnp.where(
                hit, jnp.broadcast_to(low[k : k + 1, :], (cap, tokens)), 0
            ).astype(jnp.float32).astype(jnp.bfloat16)

    pending = []
    sources = (fwd_in, saved_in, grad_in)

    def dispatch(t, k):
        return pltpu.make_async_remote_copy(
            src_ref=packed.at[t, pl.ds(k * cap, cap)],
            dst_ref=slots.at[t, pl.ds(k * cap, cap)],
            send_sem=disp_s.at[t, k],
            recv_sem=disp_r.at[t, k],
            device_id=expert_peer(k),
            device_id_type=MESH,
        )

    def pack(t):
        way = 0 if t == 0 else 1
        rows = jnp.dot(pick[way], sources[t][0], preferred_element_type=jnp.float32)
        rows = rows.astype(jnp.bfloat16)
        slots[t, pl.ds(0, cap), :] = rows[:cap]
        packed[t, pl.ds(cap, (group - 1) * cap), :] = rows[cap:]

    pack(1)
    pack(2)
    pl.semaphore_wait(barrier, len(peers))
    for k in range(1, group):
        for t in (1, 2):
            copy = dispatch(t, k)
            copy.start()
            pending.append(copy)
    pack(0)
    for k in range(1, group):
        copy = dispatch(0, k)
        copy.start()
        pending.append(copy)

    def part_copy(t, g, k):
        peer = lax.rem(mine + k, shards)
        return pltpu.make_async_remote_copy(
            src_ref=part_out.at[t, peer, pl.ds(g * span, span)],
            dst_ref=part_in.at[t, k - 1, pl.ds(g * span, span)],
            send_sem=part_s.at[t, g, k - 1],
            recv_sem=part_r.at[t, g, k - 1],
            device_id=shard_peer(k),
            device_id_type=MESH,
        )

    def act_copy(way, g, k):
        return pltpu.make_async_remote_copy(
            src_ref=act.at[way, mine, pl.ds(g * span, span)],
            dst_ref=act.at[way, mine, pl.ds(g * span, span)],
            send_sem=act_s.at[way, g, k - 1],
            recv_sem=act_r.at[way, g, k - 1],
            device_id=shard_peer(k),
            device_id_type=MESH,
        )

    def send_parts(t, g):
        for k in range(1, shards):
            copy = part_copy(t, g, k)
            copy.start()
            pending.append(copy)

    def arrive(t, g):
        for b in range(per_group):
            k = g * per_group + b
            if k > 0:
                dispatch(t, k).wait_recv()

    def partial(t, g):
        rows = pl.ds(g * span, span)
        arrive(t, g)

        @pl.loop(0, shards)
        def _(q):
            cols = pl.ds(pl.multiple_of(q * quarter, quarter), quarter)
            if t == 2:
                value = lax.dot_general(
                    slots[t, rows, :], w_out[cols, :], (((1,), (1,)), ((), ())),
                    preferred_element_type=jnp.float32)
            else:
                value = jnp.dot(slots[t, rows, :], w_in[:, cols],
                                preferred_element_type=jnp.float32)
            part_out[t, q, rows, :] = value.astype(jnp.bfloat16)

        send_parts(t, g)

    def total(t, g):
        rows = pl.ds(g * span, span)
        value = part_out[t, mine, rows, :].astype(jnp.float32)
        for k in range(1, shards):
            part_copy(t, g, k).wait_recv()
            value = value + part_in[t, k - 1, rows, :].astype(jnp.float32)
        return value

    def send_act(way, g, value):
        act[way, mine, pl.ds(g * span, span), :] = value.astype(jnp.bfloat16)
        for k in range(1, shards):
            copy = act_copy(way, g, k)
            copy.start()
            pending.append(copy)

    def forward_act(g):
        hidden = total(0, g)
        send_act(0, g, hidden / (1.0 + jnp.exp(-hidden)))

    def backward_act(g):
        hidden = total(1, g)
        slope = total(2, g)
        squash = 1.0 / (1.0 + jnp.exp(-hidden))
        send_act(1, g, slope * squash * (1.0 + hidden * (1.0 - squash)))

    def ret_copy(way, c, k):
        start, size = chunks[c]
        view = (way, pl.ds(k * cap, cap), pl.ds(start, size))
        return pltpu.make_async_remote_copy(
            src_ref=ret_out.at[view],
            dst_ref=ret_in.at[view],
            send_sem=ret_s.at[way, c, k],
            recv_sem=ret_r.at[way, c, k],
            device_id=(sec, lax.rem(me - k + group, group), mine),
            device_id_type=MESH,
        )

    def give_back(way):
        for g in range(groups):
            for k in range(1, shards):
                act_copy(way, g, k).wait_recv()
        for c, (start, size) in enumerate(chunks):
            cols = pl.ds(start, size)
            value = None
            for q in range(shards):
                units = pl.ds(q * quarter, quarter)
                if way == 0:
                    term = jnp.dot(act[way, q], w_out[units, cols],
                                   preferred_element_type=jnp.float32)
                else:
                    term = lax.dot_general(
                        act[way, q], w_in[cols, units], (((1,), (1,)), ((), ())),
                        preferred_element_type=jnp.float32)
                value = term if value is None else value + term
            value = value.astype(jnp.bfloat16)
            ret_in[way, pl.ds(0, cap), cols] = value[:cap]
            ret_out[way, pl.ds(cap, (group - 1) * cap), cols] = value[cap:]
            for k in range(1, group):
                copy = ret_copy(way, c, k)
                copy.start()
                pending.append(copy)

    def hop_copy(way, c):
        start, size = chunks[c]
        out = fwd_out if way == 0 else bwd_out
        return pltpu.make_async_remote_copy(
            src_ref=done.at[way, :, pl.ds(start, size)],
            dst_ref=out.at[0, :, pl.ds(start, size)],
            send_sem=hop_s.at[way, c],
            recv_sem=hop_r.at[way, c],
            device_id=section_peer(1 if way == 0 else -1),
            device_id_type=MESH,
        )

    def mix(way):
        tok = fwd_in if way == 0 else grad_in
        over = (((0,), (0,)), ((), ()))
        for c, (start, size) in enumerate(chunks):
            cols = pl.ds(start, size)
            for k in range(1, group):
                ret_copy(way, c, k).wait_recv()
            back = ret_in[way, :, cols]
            high = lax.dot_general(mix_hi[way], back, over, preferred_element_type=jnp.float32)
            low = lax.dot_general(mix_lo[way], back, over, preferred_element_type=jnp.float32)
            summed = (high * 256.0 + low) * (1.0 / 32768.0)
            done[way, :, cols] = (tok[0, :, cols].astype(jnp.float32) + summed).astype(
                jnp.bfloat16)
            copy = hop_copy(way, c)
            copy.start()
            pending.append(copy)

    load_in.wait()
    load_out.wait()
    last = groups - 1
    for g in range(groups):
        partial(1, g)
        partial(2, g)
        if g < last:
            backward_act(g)
    partial(0, 0)
    backward_act(last)
    if groups > 1:
        partial(0, 1)
    give_back(1)
    forward_act(0)
    for g in range(2, groups):
        partial(0, g)
        forward_act(g - 1)
    if groups > 1:
        forward_act(last)
    give_back(0)
    mix(1)
    mix(0)
    for way in (1, 0):
        for c in range(len(chunks)):
            hop_copy(way, c).wait_recv()
    for copy in pending:
        copy.wait_send()


def per_device(dims_base, fwd_in, saved_in, grad_in, w_in, w_out, ids_fwd, weight_fwd, ids_bwd,
               weight_bwd):
    sections, group, shards = dims_base
    tokens, features = fwd_in.shape[1:]
    hidden = w_in.shape[3]
    assert w_in.shape[:2] == (1, 1)
    top = ids_fwd.shape[2]
    assert top == 2
    room = max(2, (tokens * top * 5 + 4 * group - 1) // (4 * group))
    cap = -(-room // ROWS) * ROWS
    groups = 4 if group % 4 == 0 else 1
    quarter = hidden // shards
    rows = group * cap
    nc = len(column_chunks(features))
    dims = (sections, group, shards, cap, tokens, features, quarter, groups)
    meta = jnp.concatenate(
        [ids_fwd[0].T, weight_fwd[0].T, ids_bwd[0].T, weight_bwd[0].T], axis=0)
    bf = jnp.bfloat16
    dma = pltpu.SemaphoreType.DMA
    vmem = pl.BlockSpec(memory_space=pltpu.VMEM)
    anywhere = pl.BlockSpec(memory_space=pl.ANY)
    out = jax.ShapeDtypeStruct(fwd_in.shape, bf)
    return pl.pallas_call(
        functools.partial(kernel, dims),
        name="relay",
        out_shape=(out, out),
        in_specs=[vmem] * 4 + [anywhere] * 2,
        out_specs=(vmem, vmem),
        scratch_shapes=[
            pltpu.VMEM((features, hidden), bf),
            pltpu.VMEM((hidden, features), bf),
            pltpu.VMEM((2, rows, tokens), bf),
            pltpu.VMEM((2, rows, tokens), bf),
            pltpu.VMEM((2, rows, tokens), bf),
            pltpu.VMEM((3, rows, features), bf),
            pltpu.VMEM((3, rows, features), bf),
            pltpu.VMEM((3, shards, rows, quarter), bf),
            pltpu.VMEM((3, shards - 1, rows, quarter), bf),
            pltpu.VMEM((2, shards, rows, quarter), bf),
            pltpu.VMEM((2, rows, features), bf),
            pltpu.VMEM((2, rows, features), bf),
            pltpu.VMEM((2, tokens, features), bf),
            dma((2,)),
            dma((3, group)), dma((3, group)),
            dma((3, groups, shards - 1)), dma((3, groups, shards - 1)),
            dma((2, groups, shards - 1)), dma((2, groups, shards - 1)),
            dma((2, nc, group)), dma((2, nc, group)),
            dma((2, nc)), dma((2, nc)),
        ],
        compiler_params=pltpu.CompilerParams(
            collective_id=0, has_side_effects=True, vmem_limit_bytes=56 * 2**20),
    )(meta, fwd_in, saved_in, grad_in, w_in, w_out)


def solution(mesh):
    rows = P("section", "expert", "shard")
    slots = P("section", "expert", None)
    dims_base = (mesh.shape["section"], mesh.shape["expert"], mesh.shape["shard"])
    return jax.shard_map(
        functools.partial(per_device, dims_base),
        mesh=mesh,
        in_specs=(rows, rows, rows, P("section", "expert", "shard", None),
                  P("section", "expert", None, "shard"), slots, slots, slots, slots),
        out_specs=(rows, rows),
        check_vma=False,
    )
```

```python
import functools

import jax
import jax.numpy as jnp
from jax import lax
from jax.experimental import pallas as pl
from jax.experimental.pallas import tpu as pltpu
from jax.sharding import PartitionSpec as P

MESH = pl.DeviceIdType.MESH
LANES = 128
ROWS = 16


def column_chunks(features):
    chunks, start = [], 0
    while start < features:
        size = min(3 * LANES, features - start)
        chunks.append((start, size))
        start += size
    return chunks


def kernel(dims, meta, fwd_in, saved_in, grad_in, w_in_hbm, w_out_hbm, fwd_out, bwd_out,
           w_in, w_out, pick, mix_hi, mix_lo, packed, slots, part_out, part_in, act,
           ret_out, ret_in, done, w_sem, disp_s, disp_r, part_s, part_r, act_s, act_r,
           ret_s, ret_r, hop_s, hop_r):
    sections, group, shards, cap, tokens, features, quarter, groups = dims
    per_group = group // groups
    span = per_group * cap
    chunks = column_chunks(features)
    sec = lax.axis_index("section")
    me = lax.axis_index("expert")
    mine = lax.axis_index("shard")

    load_in = pltpu.make_async_copy(w_in_hbm.at[0, 0], w_in, w_sem.at[0])
    load_out = pltpu.make_async_copy(w_out_hbm.at[0, 0], w_out, w_sem.at[1])
    load_in.start()
    load_out.start()

    def expert_peer(k):
        return (sec, lax.rem(me + k, group), mine)

    def shard_peer(k):
        return (sec, me, lax.rem(mine + k, shards))

    def section_peer(k):
        return (lax.rem(sec + k + sections, sections), me, mine)

    barrier = pltpu.get_barrier_semaphore()
    peers = [expert_peer(k) for k in range(1, group)]
    peers += [shard_peer(k) for k in range(1, shards)]
    peers += [section_peer(1), section_peer(-1)]
    for peer in peers:
        pl.semaphore_signal(barrier, inc=1, device_id=peer, device_id_type=MESH)

    upper = (lax.broadcasted_iota(jnp.int32, (tokens, tokens), 0)
             < lax.broadcasted_iota(jnp.int32, (tokens, tokens), 1)).astype(jnp.bfloat16)
    height = max(group, 8)
    labels = lax.rem(lax.broadcasted_iota(jnp.int32, (height, tokens), 0) + me, group)
    spots = lax.broadcasted_iota(jnp.int32, (cap, tokens), 0)
    for way in range(2):
        base = 4 * way
        first = jnp.broadcast_to(meta[base : base + 1, :], (height, tokens)) == labels
        second = jnp.broadcast_to(meta[base + 1 : base + 2, :], (height, tokens)) == labels
        q_first = jnp.broadcast_to(meta[base + 2 : base + 3, :], (height, tokens))
        q_second = jnp.broadcast_to(meta[base + 3 : base + 4, :], (height, tokens))
        weight = jnp.where(first, q_first, 0) + jnp.where(second, q_second, 0)
        named = jnp.where(first, 1, 0) + jnp.where(second, 1, 0)
        rank = jnp.dot(named.astype(jnp.float32).astype(jnp.bfloat16), upper,
                       preferred_element_type=jnp.float32).astype(jnp.int32)
        spot = jnp.where(named > 0, rank, cap)
        high = weight >> 8
        low = weight & 255
        for k in range(group):
            hit = jnp.broadcast_to(spot[k : k + 1, :], (cap, tokens)) == spots
            rows = pl.ds(k * cap, cap)
            pick[way, rows, :] = jnp.where(hit, 1.0, 0.0).astype(jnp.bfloat16)
            mix_hi[way, rows, :] = jnp.where(
                hit, jnp.broadcast_to(high[k : k + 1, :], (cap, tokens)), 0
            ).astype(jnp.float32).astype(jnp.bfloat16)
            mix_lo[way, rows, :] = jnp.where(
                hit, jnp.broadcast_to(low[k : k + 1, :], (cap, tokens)), 0
            ).astype(jnp.float32).astype(jnp.bfloat16)

    pending = []
    sources = (fwd_in, saved_in, grad_in)

    def dispatch(t, k):
        return pltpu.make_async_remote_copy(
            src_ref=packed.at[t, pl.ds(k * cap, cap)],
            dst_ref=slots.at[t, pl.ds(k * cap, cap)],
            send_sem=disp_s.at[t, k],
            recv_sem=disp_r.at[t, k],
            device_id=expert_peer(k),
            device_id_type=MESH,
        )

    def pack(t):
        way = 0 if t == 0 else 1
        rows = jnp.dot(pick[way], sources[t][0], preferred_element_type=jnp.float32)
        rows = rows.astype(jnp.bfloat16)
        slots[t, pl.ds(0, cap), :] = rows[:cap]
        packed[t, pl.ds(cap, (group - 1) * cap), :] = rows[cap:]

    def blocks(g):
        return [k for k in range(g * per_group, (g + 1) * per_group) if k > 0]

    def issue(tensors, g):
        for k in blocks(g):
            for t in tensors:
                dispatch(t, k).start()

    def drain(tensors, g):
        for k in blocks(g):
            for t in tensors:
                dispatch(t, k).wait_send()

    pack(1)
    pack(2)
    pl.semaphore_wait(barrier, len(peers))
    queue = [(t, g) for t in ((1, 2), (0,)) for g in range(groups) if blocks(g)]
    sent = min(2, len(queue))
    for item in queue[:sent]:
        issue(*item)
    pack(0)

    def part_copy(t, g, k):
        peer = lax.rem(mine + k, shards)
        return pltpu.make_async_remote_copy(
            src_ref=part_out.at[t, peer, pl.ds(g * span, span)],
            dst_ref=part_in.at[t, k - 1, pl.ds(g * span, span)],
            send_sem=part_s.at[t, g, k - 1],
            recv_sem=part_r.at[t, g, k - 1],
            device_id=shard_peer(k),
            device_id_type=MESH,
        )

    def act_copy(way, g, k):
        return pltpu.make_async_remote_copy(
            src_ref=act.at[way, mine, pl.ds(g * span, span)],
            dst_ref=act.at[way, mine, pl.ds(g * span, span)],
            send_sem=act_s.at[way, g, k - 1],
            recv_sem=act_r.at[way, g, k - 1],
            device_id=shard_peer(k),
            device_id_type=MESH,
        )

    def send_parts(t, g):
        for k in range(1, shards):
            copy = part_copy(t, g, k)
            copy.start()
            pending.append(copy)

    def arrive(t, g):
        for b in range(per_group):
            k = g * per_group + b
            if k > 0:
                dispatch(t, k).wait_recv()

    def partial(t, g):
        rows = pl.ds(g * span, span)
        arrive(t, g)

        @pl.loop(0, shards)
        def _(q):
            cols = pl.ds(pl.multiple_of(q * quarter, quarter), quarter)
            if t == 2:
                value = lax.dot_general(
                    slots[t, rows, :], w_out[cols, :], (((1,), (1,)), ((), ())),
                    preferred_element_type=jnp.float32)
            else:
                value = jnp.dot(slots[t, rows, :], w_in[:, cols],
                                preferred_element_type=jnp.float32)
            part_out[t, q, rows, :] = value.astype(jnp.bfloat16)

        send_parts(t, g)

    def total(t, g):
        rows = pl.ds(g * span, span)
        value = part_out[t, mine, rows, :].astype(jnp.float32)
        for k in range(1, shards):
            part_copy(t, g, k).wait_recv()
            value = value + part_in[t, k - 1, rows, :].astype(jnp.float32)
        return value

    def send_act(way, g, value):
        act[way, mine, pl.ds(g * span, span), :] = value.astype(jnp.bfloat16)
        for k in range(1, shards):
            copy = act_copy(way, g, k)
            copy.start()
            pending.append(copy)

    def forward_act(g):
        hidden = total(0, g)
        send_act(0, g, hidden / (1.0 + jnp.exp(-hidden)))

    def backward_act(g):
        hidden = total(1, g)
        slope = total(2, g)
        squash = 1.0 / (1.0 + jnp.exp(-hidden))
        send_act(1, g, slope * squash * (1.0 + hidden * (1.0 - squash)))

    def ret_copy(way, c, k):
        start, size = chunks[c]
        view = (way, pl.ds(k * cap, cap), pl.ds(start, size))
        return pltpu.make_async_remote_copy(
            src_ref=ret_out.at[view],
            dst_ref=ret_in.at[view],
            send_sem=ret_s.at[way, c, k],
            recv_sem=ret_r.at[way, c, k],
            device_id=(sec, lax.rem(me - k + group, group), mine),
            device_id_type=MESH,
        )

    def give_back(way, ahead):
        for g in range(groups):
            for k in range(1, shards):
                act_copy(way, g, k).wait_recv()
        for c, (start, size) in enumerate(chunks):
            cols = pl.ds(start, size)
            value = None
            for q in range(shards):
                units = pl.ds(q * quarter, quarter)
                if way == 0:
                    term = jnp.dot(act[way, q], w_out[units, cols],
                                   preferred_element_type=jnp.float32)
                else:
                    term = lax.dot_general(
                        act[way, q], w_in[cols, units], (((1,), (1,)), ((), ())),
                        preferred_element_type=jnp.float32)
                value = term if value is None else value + term
            value = value.astype(jnp.bfloat16)
            ret_in[way, pl.ds(0, cap), cols] = value[:cap]
            ret_out[way, pl.ds(cap, (group - 1) * cap), cols] = value[cap:]
            for k in range(1, group):
                if c >= ahead:
                    ret_copy(way, c - ahead, k).wait_send()
                ret_copy(way, c, k).start()
        for c in range(max(0, len(chunks) - ahead), len(chunks)):
            pending.extend(ret_copy(way, c, k) for k in range(1, group))

    def hop_copy(way, c):
        start, size = chunks[c]
        out = fwd_out if way == 0 else bwd_out
        return pltpu.make_async_remote_copy(
            src_ref=done.at[way, :, pl.ds(start, size)],
            dst_ref=out.at[0, :, pl.ds(start, size)],
            send_sem=hop_s.at[way, c],
            recv_sem=hop_r.at[way, c],
            device_id=section_peer(1 if way == 0 else -1),
            device_id_type=MESH,
        )

    def mix(way):
        tok = fwd_in if way == 0 else grad_in
        over = (((0,), (0,)), ((), ()))
        for c, (start, size) in enumerate(chunks):
            cols = pl.ds(start, size)
            for k in range(1, group):
                ret_copy(way, c, k).wait_recv()
            back = ret_in[way, :, cols]
            high = lax.dot_general(mix_hi[way], back, over, preferred_element_type=jnp.float32)
            low = lax.dot_general(mix_lo[way], back, over, preferred_element_type=jnp.float32)
            summed = (high * 256.0 + low) * (1.0 / 32768.0)
            done[way, :, cols] = (tok[0, :, cols].astype(jnp.float32) + summed).astype(
                jnp.bfloat16)
            copy = hop_copy(way, c)
            copy.start()
            pending.append(copy)

    load_in.wait()
    load_out.wait()
    last = groups - 1
    for g in range(groups):
        partial(1, g)
        partial(2, g)
        drain((1, 2), g)
        if blocks(g) and sent < len(queue):
            issue(*queue[sent])
            sent += 1
        if g < last:
            backward_act(g)
    for item in queue[sent:]:
        issue(*item)
    partial(0, 0)
    backward_act(last)
    if groups > 1:
        partial(0, 1)
    give_back(1, len(chunks))
    forward_act(0)
    for g in range(2, groups):
        partial(0, g)
        forward_act(g - 1)
    if groups > 1:
        forward_act(last)
    for g in range(groups):
        drain((0,), g)
    give_back(0, 2)
    mix(1)
    mix(0)
    for way in (1, 0):
        for c in range(len(chunks)):
            hop_copy(way, c).wait_recv()
    for copy in pending:
        copy.wait_send()


def settle(fwd, bwd, fwd_out, bwd_out, rows, sem):
    loads = [pltpu.make_async_copy(ref, rows.at[i], sem.at[0, i])
             for i, ref in enumerate((fwd, bwd))]
    stores = [pltpu.make_async_copy(rows.at[i], ref, sem.at[1, i])
              for i, ref in enumerate((fwd_out, bwd_out))]
    for load in loads:
        load.start()
    for load, store in zip(loads, stores):
        load.wait()
        store.start()
    for store in stores:
        store.wait()


def per_device(dims_base, fwd_in, saved_in, grad_in, w_in, w_out, ids_fwd, weight_fwd, ids_bwd,
               weight_bwd):
    sections, group, shards = dims_base
    tokens, features = fwd_in.shape[1:]
    hidden = w_in.shape[3]
    assert w_in.shape[:2] == (1, 1)
    top = ids_fwd.shape[2]
    assert top == 2
    room = max(2, (tokens * top * 5 + 4 * group - 1) // (4 * group))
    cap = -(-room // ROWS) * ROWS
    groups = 4 if group % 4 == 0 else 1
    quarter = hidden // shards
    rows = group * cap
    nc = len(column_chunks(features))
    dims = (sections, group, shards, cap, tokens, features, quarter, groups)
    meta = jnp.concatenate(
        [ids_fwd[0].T, weight_fwd[0].T, ids_bwd[0].T, weight_bwd[0].T], axis=0)
    bf = jnp.bfloat16
    dma = pltpu.SemaphoreType.DMA
    vmem = pl.BlockSpec(memory_space=pltpu.VMEM)
    anywhere = pl.BlockSpec(memory_space=pl.ANY)
    out = jax.ShapeDtypeStruct(fwd_in.shape, bf)
    fwd, bwd = pl.pallas_call(
        functools.partial(kernel, dims),
        name="relay",
        out_shape=(out, out),
        in_specs=[vmem] * 4 + [anywhere] * 2,
        out_specs=(vmem, vmem),
        scratch_shapes=[
            pltpu.VMEM((features, hidden), bf),
            pltpu.VMEM((hidden, features), bf),
            pltpu.VMEM((2, rows, tokens), bf),
            pltpu.VMEM((2, rows, tokens), bf),
            pltpu.VMEM((2, rows, tokens), bf),
            pltpu.VMEM((3, rows, features), bf),
            pltpu.VMEM((3, rows, features), bf),
            pltpu.VMEM((3, shards, rows, quarter), bf),
            pltpu.VMEM((3, shards - 1, rows, quarter), bf),
            pltpu.VMEM((2, shards, rows, quarter), bf),
            pltpu.VMEM((2, rows, features), bf),
            pltpu.VMEM((2, rows, features), bf),
            pltpu.VMEM((2, tokens, features), bf),
            dma((2,)),
            dma((3, group)), dma((3, group)),
            dma((3, groups, shards - 1)), dma((3, groups, shards - 1)),
            dma((2, groups, shards - 1)), dma((2, groups, shards - 1)),
            dma((2, nc, group)), dma((2, nc, group)),
            dma((2, nc)), dma((2, nc)),
        ],
        compiler_params=pltpu.CompilerParams(
            collective_id=0, has_side_effects=True, vmem_limit_bytes=56 * 2**20),
    )(meta, fwd_in, saved_in, grad_in, w_in, w_out)
    return pl.pallas_call(
        settle,
        name="settle",
        out_shape=(out, out),
        in_specs=[anywhere] * 2,
        out_specs=(anywhere, anywhere),
        scratch_shapes=[pltpu.VMEM((2,) + fwd_in.shape, bf), dma((2, 2))],
    )(fwd, bwd)


def solution(mesh):
    rows = P("section", "expert", "shard")
    slots = P("section", "expert", None)
    dims_base = (mesh.shape["section"], mesh.shape["expert"], mesh.shape["shard"])
    return jax.shard_map(
        functools.partial(per_device, dims_base),
        mesh=mesh,
        in_specs=(rows, rows, rows, P("section", "expert", "shard", None),
                  P("section", "expert", None, "shard"), slots, slots, slots, slots),
        out_specs=(rows, rows),
        check_vma=False,
    )
```

```python
import functools

import jax
import jax.numpy as jnp
from jax import lax
from jax.experimental import pallas as pl
from jax.experimental.pallas import tpu as pltpu
from jax.sharding import PartitionSpec as P

MESH = pl.DeviceIdType.MESH
LANES = 128
ROWS = 16


def column_chunks(features):
    chunks, start = [], 0
    while start < features:
        size = min(2 * LANES, features - start)
        chunks.append((start, size))
        start += size
    return chunks


def kernel(dims, ids_fwd, q_fwd, ids_bwd, q_bwd, fwd_in, saved_in, grad_in, w_in_hbm, w_out_hbm, fwd_out, bwd_out,
           w_in, w_out, pick, mix_hi, mix_lo, packed, slots, part_out, part_in, act,
           ret_out, ret_in, done, w_sem, disp_s, disp_r, part_s, part_r, act_s, act_r,
           ret_s, ret_r, hop_s, hop_r):
    sections, group, shards, cap, tokens, features, quarter, groups = dims
    per_group = group // groups
    span = per_group * cap
    chunks = column_chunks(features)
    sec = lax.axis_index("section")
    me = lax.axis_index("expert")
    mine = lax.axis_index("shard")

    load_in = pltpu.make_async_copy(w_in_hbm.at[0, 0], w_in, w_sem.at[0])
    load_out = pltpu.make_async_copy(w_out_hbm.at[0, 0], w_out, w_sem.at[1])
    load_in.start()
    load_out.start()

    def expert_peer(k):
        return (sec, lax.rem(me + k, group), mine)

    def shard_peer(k):
        return (sec, me, lax.rem(mine + k, shards))

    def section_peer(k):
        return (lax.rem(sec + k + sections, sections), me, mine)

    barrier = pltpu.get_barrier_semaphore()
    peers = [expert_peer(k) for k in range(1, group)]
    peers += [shard_peer(k) for k in range(1, shards)]
    peers += [section_peer(1), section_peer(-1)]
    for peer in peers:
        pl.semaphore_signal(barrier, inc=1, device_id=peer, device_id_type=MESH)

    upper = (lax.broadcasted_iota(jnp.int32, (tokens, tokens), 0)
             < lax.broadcasted_iota(jnp.int32, (tokens, tokens), 1)).astype(jnp.bfloat16)
    height = max(group, 8)
    labels = lax.rem(lax.broadcasted_iota(jnp.int32, (height, tokens), 0) + me, group)
    spots = lax.broadcasted_iota(jnp.int32, (cap, tokens), 0)
    over = (height, tokens)

    def find(way):
        ids = ids_fwd if way == 0 else ids_bwd
        first = jnp.broadcast_to(ids[0:1, :], over) == labels
        second = jnp.broadcast_to(ids[1:2, :], over) == labels
        named = jnp.where(first, 1, 0) + jnp.where(second, 1, 0)
        rank = jnp.dot(named.astype(jnp.float32).astype(jnp.bfloat16), upper,
                       preferred_element_type=jnp.float32).astype(jnp.int32)
        spot = jnp.where(named > 0, rank, cap)
        for k in range(group):
            hit = jnp.broadcast_to(spot[k : k + 1, :], (cap, tokens)) == spots
            pick[way, pl.ds(k * cap, cap), :] = jnp.where(hit, 1.0, 0.0).astype(jnp.bfloat16)
        return first, second

    def weigh(way, found):
        first, second = found
        q = q_fwd if way == 0 else q_bwd
        weight = jnp.where(first, jnp.broadcast_to(q[0:1, :], over), 0) + jnp.where(
            second, jnp.broadcast_to(q[1:2, :], over), 0)
        high = (weight >> 8).astype(jnp.float32).astype(jnp.bfloat16)
        low = (weight & 255).astype(jnp.float32).astype(jnp.bfloat16)
        for k in range(group):
            rows = pl.ds(k * cap, cap)
            hit = pick[way, rows, :]
            mix_hi[way, rows, :] = hit * jnp.broadcast_to(high[k : k + 1, :], (cap, tokens))
            mix_lo[way, rows, :] = hit * jnp.broadcast_to(low[k : k + 1, :], (cap, tokens))

    pending = []
    sources = (fwd_in, saved_in, grad_in)

    def dispatch(t, k):
        return pltpu.make_async_remote_copy(
            src_ref=packed.at[t, pl.ds(k * cap, cap)],
            dst_ref=slots.at[t, pl.ds(k * cap, cap)],
            send_sem=disp_s.at[t, k],
            recv_sem=disp_r.at[t, k],
            device_id=expert_peer(k),
            device_id_type=MESH,
        )

    def pack(t):
        way = 0 if t == 0 else 1
        rows = jnp.dot(pick[way], sources[t][0], preferred_element_type=jnp.float32)
        rows = rows.astype(jnp.bfloat16)
        slots[t, pl.ds(0, cap), :] = rows[:cap]
        packed[t, pl.ds(cap, (group - 1) * cap), :] = rows[cap:]

    def blocks(g):
        return [k for k in range(g * per_group, (g + 1) * per_group) if k > 0]

    def issue(tensors, g):
        for k in blocks(g):
            for t in tensors:
                dispatch(t, k).start()

    def drain(tensors, g):
        for k in blocks(g):
            for t in tensors:
                dispatch(t, k).wait_send()

    found_bwd = find(1)
    pack(1)
    pack(2)
    pl.semaphore_wait(barrier, len(peers))
    queue = [(t, g) for t in ((1, 2), (0,)) for g in range(groups) if blocks(g)]
    sent = min(2, len(queue))
    for item in queue[:sent]:
        issue(*item)
    found_fwd = find(0)
    pack(0)
    weigh(1, found_bwd)
    weigh(0, found_fwd)

    def part_copy(t, g, k):
        peer = lax.rem(mine + k, shards)
        return pltpu.make_async_remote_copy(
            src_ref=part_out.at[t, peer, pl.ds(g * span, span)],
            dst_ref=part_in.at[t, k - 1, pl.ds(g * span, span)],
            send_sem=part_s.at[t, g, k - 1],
            recv_sem=part_r.at[t, g, k - 1],
            device_id=shard_peer(k),
            device_id_type=MESH,
        )

    def act_copy(way, g, k):
        return pltpu.make_async_remote_copy(
            src_ref=act.at[way, mine, pl.ds(g * span, span)],
            dst_ref=act.at[way, mine, pl.ds(g * span, span)],
            send_sem=act_s.at[way, g, k - 1],
            recv_sem=act_r.at[way, g, k - 1],
            device_id=shard_peer(k),
            device_id_type=MESH,
        )

    def send_parts(t, g):
        for k in range(1, shards):
            copy = part_copy(t, g, k)
            copy.start()
            pending.append(copy)

    def arrive(t, g):
        for b in range(per_group):
            k = g * per_group + b
            if k > 0:
                dispatch(t, k).wait_recv()

    def partial(t, g):
        rows = pl.ds(g * span, span)
        arrive(t, g)

        @pl.loop(0, shards)
        def _(q):
            cols = pl.ds(pl.multiple_of(q * quarter, quarter), quarter)
            if t == 2:
                value = lax.dot_general(
                    slots[t, rows, :], w_out[cols, :], (((1,), (1,)), ((), ())),
                    preferred_element_type=jnp.float32)
            else:
                value = jnp.dot(slots[t, rows, :], w_in[:, cols],
                                preferred_element_type=jnp.float32)
            part_out[t, q, rows, :] = value.astype(jnp.bfloat16)

        send_parts(t, g)

    def total(t, g):
        rows = pl.ds(g * span, span)
        value = part_out[t, mine, rows, :].astype(jnp.float32)
        for k in range(1, shards):
            part_copy(t, g, k).wait_recv()
            value = value + part_in[t, k - 1, rows, :].astype(jnp.float32)
        return value

    def send_act(way, g, value):
        act[way, mine, pl.ds(g * span, span), :] = value.astype(jnp.bfloat16)
        for k in range(1, shards):
            copy = act_copy(way, g, k)
            copy.start()
            pending.append(copy)

    def forward_act(g):
        hidden = total(0, g)
        send_act(0, g, hidden / (1.0 + jnp.exp(-hidden)))

    def backward_act(g):
        hidden = total(1, g)
        slope = total(2, g)
        squash = 1.0 / (1.0 + jnp.exp(-hidden))
        send_act(1, g, slope * squash * (1.0 + hidden * (1.0 - squash)))

    def ret_copy(way, c, k):
        start, size = chunks[c] if way == 0 else (0, features)
        view = (way, pl.ds(k * cap, cap), pl.ds(start, size))
        return pltpu.make_async_remote_copy(
            src_ref=ret_out.at[view],
            dst_ref=ret_in.at[view],
            send_sem=ret_s.at[way, c, k],
            recv_sem=ret_r.at[way, c, k],
            device_id=(sec, lax.rem(me - k + group, group), mine),
            device_id_type=MESH,
        )

    def rows_back(g):
        for k in range(1, shards):
            act_copy(1, g, k).wait_recv()
        value = None
        for q in range(shards):
            term = lax.dot_general(
                act[1, q, pl.ds(g * span, span), :], w_in[:, pl.ds(q * quarter, quarter)],
                (((1,), (1,)), ((), ())), preferred_element_type=jnp.float32)
            value = term if value is None else value + term
        value = value.astype(jnp.bfloat16)
        for b in range(per_group):
            k = g * per_group + b
            target = ret_in if k == 0 else ret_out
            target[1, pl.ds(k * cap, cap), :] = value[b * cap : (b + 1) * cap]

    def send_back(g):
        for k in blocks(g):
            copy = ret_copy(1, 0, k)
            copy.start()
            pending.append(copy)

    def give_back(ahead):
        for g in range(groups):
            for k in range(1, shards):
                act_copy(0, g, k).wait_recv()
        for c, (start, size) in enumerate(chunks):
            cols = pl.ds(start, size)
            value = None
            for q in range(shards):
                term = jnp.dot(act[0, q], w_out[pl.ds(q * quarter, quarter), cols],
                               preferred_element_type=jnp.float32)
                value = term if value is None else value + term
            value = value.astype(jnp.bfloat16)
            ret_in[0, pl.ds(0, cap), cols] = value[:cap]
            ret_out[0, pl.ds(cap, (group - 1) * cap), cols] = value[cap:]
            if c < ahead:
                for k in range(1, group):
                    ret_copy(0, c, k).start()

    def follow(c):
        for k in range(1, group):
            ret_copy(0, c, k).wait_send()
        if c + 2 < len(chunks):
            for k in range(1, group):
                ret_copy(0, c + 2, k).start()

    def hop_copy(way, c):
        start, size = chunks[c]
        out = fwd_out if way == 0 else bwd_out
        return pltpu.make_async_remote_copy(
            src_ref=done.at[way, :, pl.ds(start, size)],
            dst_ref=out.at[0, :, pl.ds(start, size)],
            send_sem=hop_s.at[way, c],
            recv_sem=hop_r.at[way, c],
            device_id=section_peer(1 if way == 0 else -1),
            device_id_type=MESH,
        )

    def mix(way, c):
        tok = fwd_in if way == 0 else grad_in
        across = (((0,), (0,)), ((), ()))
        start, size = chunks[c]
        cols = pl.ds(start, size)
        if way == 0 or c == 0:
            for k in range(1, group):
                ret_copy(way, c, k).wait_recv()
        back = ret_in[way, :, cols]
        high = lax.dot_general(mix_hi[way], back, across, preferred_element_type=jnp.float32)
        low = lax.dot_general(mix_lo[way], back, across, preferred_element_type=jnp.float32)
        summed = (high * 256.0 + low) * (1.0 / 32768.0)
        done[way, :, cols] = (tok[0, :, cols].astype(jnp.float32) + summed).astype(jnp.bfloat16)
        copy = hop_copy(way, c)
        copy.start()
        pending.append(copy)

    load_in.wait()
    load_out.wait()
    last = groups - 1
    for g in range(groups):
        partial(1, g)
        partial(2, g)
        drain((1, 2), g)
        if blocks(g) and sent < len(queue):
            issue(*queue[sent])
            sent += 1
        if g < last:
            backward_act(g)
            if g > 0:
                rows_back(g - 1)
    for item in queue[sent:]:
        issue(*item)
    partial(0, 0)
    backward_act(last)
    if last > 0:
        rows_back(last - 1)
    for g in range(groups):
        if g > 0:
            partial(0, g)
        drain((0,), g)
        if g > 0:
            send_back(g - 1)
            forward_act(g - 1)
    rows_back(last)
    send_back(last)
    forward_act(last)
    give_back(2)
    for c in range(len(chunks)):
        mix(1, c)
    for c in range(len(chunks)):
        follow(c)
        mix(0, c)
    for way in (1, 0):
        for c in range(len(chunks)):
            hop_copy(way, c).wait_recv()
    for copy in pending:
        copy.wait_send()


def settle(fwd, bwd, fwd_out, bwd_out, rows, sem):
    loads = [pltpu.make_async_copy(ref, rows.at[i], sem.at[0, i])
             for i, ref in enumerate((fwd, bwd))]
    stores = [pltpu.make_async_copy(rows.at[i], ref, sem.at[1, i])
              for i, ref in enumerate((fwd_out, bwd_out))]
    for load in loads:
        load.start()
    for load, store in zip(loads, stores):
        load.wait()
        store.start()
    for store in stores:
        store.wait()


def per_device(dims_base, fwd_in, saved_in, grad_in, w_in, w_out, ids_fwd, weight_fwd, ids_bwd,
               weight_bwd):
    sections, group, shards = dims_base
    tokens, features = fwd_in.shape[1:]
    hidden = w_in.shape[3]
    assert w_in.shape[:2] == (1, 1)
    top = ids_fwd.shape[2]
    assert top == 2
    room = max(2, (tokens * top * 5 + 4 * group - 1) // (4 * group))
    cap = -(-room // ROWS) * ROWS
    groups = 4 if group % 4 == 0 else 1
    quarter = hidden // shards
    rows = group * cap
    nc = len(column_chunks(features))
    dims = (sections, group, shards, cap, tokens, features, quarter, groups)
    routing = [a[0].T for a in (ids_fwd, weight_fwd, ids_bwd, weight_bwd)]
    bf = jnp.bfloat16
    dma = pltpu.SemaphoreType.DMA
    vmem = pl.BlockSpec(memory_space=pltpu.VMEM)
    anywhere = pl.BlockSpec(memory_space=pl.ANY)
    out = jax.ShapeDtypeStruct(fwd_in.shape, bf)
    fwd, bwd = pl.pallas_call(
        functools.partial(kernel, dims),
        name="relay",
        out_shape=(out, out),
        in_specs=[vmem] * 7 + [anywhere] * 2,
        out_specs=(vmem, vmem),
        scratch_shapes=[
            pltpu.VMEM((features, hidden), bf),
            pltpu.VMEM((hidden, features), bf),
            pltpu.VMEM((2, rows, tokens), bf),
            pltpu.VMEM((2, rows, tokens), bf),
            pltpu.VMEM((2, rows, tokens), bf),
            pltpu.VMEM((3, rows, features), bf),
            pltpu.VMEM((3, rows, features), bf),
            pltpu.VMEM((3, shards, rows, quarter), bf),
            pltpu.VMEM((3, shards - 1, rows, quarter), bf),
            pltpu.VMEM((2, shards, rows, quarter), bf),
            pltpu.VMEM((2, rows, features), bf),
            pltpu.VMEM((2, rows, features), bf),
            pltpu.VMEM((2, tokens, features), bf),
            dma((2,)),
            dma((3, group)), dma((3, group)),
            dma((3, groups, shards - 1)), dma((3, groups, shards - 1)),
            dma((2, groups, shards - 1)), dma((2, groups, shards - 1)),
            dma((2, nc, group)), dma((2, nc, group)),
            dma((2, nc)), dma((2, nc)),
        ],
        compiler_params=pltpu.CompilerParams(
            collective_id=0, has_side_effects=True, vmem_limit_bytes=56 * 2**20),
    )(*routing, fwd_in, saved_in, grad_in, w_in, w_out)
    return pl.pallas_call(
        settle,
        name="settle",
        out_shape=(out, out),
        in_specs=[anywhere] * 2,
        out_specs=(anywhere, anywhere),
        scratch_shapes=[pltpu.VMEM((2,) + fwd_in.shape, bf), dma((2, 2))],
    )(fwd, bwd)


def solution(mesh):
    rows = P("section", "expert", "shard")
    slots = P("section", "expert", None)
    dims_base = (mesh.shape["section"], mesh.shape["expert"], mesh.shape["shard"])
    return jax.shard_map(
        functools.partial(per_device, dims_base),
        mesh=mesh,
        in_specs=(rows, rows, rows, P("section", "expert", "shard", None),
                  P("section", "expert", None, "shard"), slots, slots, slots, slots),
        out_specs=(rows, rows),
        check_vma=False,
    )
```

```python
import functools

import jax
import jax.numpy as jnp
from jax import lax
from jax.experimental import pallas as pl
from jax.experimental.pallas import tpu as pltpu
from jax.sharding import PartitionSpec as P

MESH = pl.DeviceIdType.MESH
LANES = 128
ROWS = 16


def column_chunks(features):
    chunks, start = [], 0
    while start < features:
        size = min(2 * LANES, features - start)
        chunks.append((start, size))
        start += size
    return chunks


def kernel(dims, ids_fwd, q_fwd, ids_bwd, q_bwd, fwd_in, saved_in, grad_in, w_in_hbm, w_out_hbm, fwd_out, bwd_out,
           w_in, w_out, pick, mix_hi, mix_lo, packed, slots, part_out, part_in, act,
           ret_out, ret_in, done, w_sem, disp_s, disp_r, part_s, part_r, act_s, act_r,
           ret_s, ret_r, hop_s, hop_r):
    sections, group, shards, cap, tokens, features, quarter, groups = dims
    per_group = group // groups
    span = per_group * cap
    chunks = column_chunks(features)
    last = groups - 1
    sec = lax.axis_index("section")
    me = lax.axis_index("expert")
    mine = lax.axis_index("shard")

    load_in = pltpu.make_async_copy(w_in_hbm.at[0, 0], w_in, w_sem.at[0])
    load_out = pltpu.make_async_copy(w_out_hbm.at[0, 0], w_out, w_sem.at[1])
    load_in.start()
    load_out.start()

    def expert_peer(k):
        return (sec, lax.rem(me + k, group), mine)

    def shard_peer(k):
        return (sec, me, lax.rem(mine + k, shards))

    def section_peer(k):
        return (lax.rem(sec + k + sections, sections), me, mine)

    barrier = pltpu.get_barrier_semaphore()
    peers = [expert_peer(k) for k in range(1, group)]
    peers += [shard_peer(k) for k in range(1, shards)]
    peers += [section_peer(1), section_peer(-1)]
    for peer in peers:
        pl.semaphore_signal(barrier, inc=1, device_id=peer, device_id_type=MESH)

    upper = (lax.broadcasted_iota(jnp.int32, (tokens, tokens), 0)
             < lax.broadcasted_iota(jnp.int32, (tokens, tokens), 1)).astype(jnp.bfloat16)
    height = max(group, 8)
    labels = lax.rem(lax.broadcasted_iota(jnp.int32, (height, tokens), 0) + me, group)
    spots = lax.broadcasted_iota(jnp.int32, (cap, tokens), 0)
    over = (height, tokens)

    def find(way):
        ids = ids_fwd if way == 0 else ids_bwd
        first = jnp.broadcast_to(ids[0:1, :], over) == labels
        second = jnp.broadcast_to(ids[1:2, :], over) == labels
        named = jnp.where(first, 1, 0) + jnp.where(second, 1, 0)
        rank = jnp.dot(named.astype(jnp.float32).astype(jnp.bfloat16), upper,
                       preferred_element_type=jnp.float32).astype(jnp.int32)
        spot = jnp.where(named > 0, rank, cap)
        for k in range(group):
            hit = jnp.broadcast_to(spot[k : k + 1, :], (cap, tokens)) == spots
            pick[way, pl.ds(k * cap, cap), :] = jnp.where(hit, 1.0, 0.0).astype(jnp.bfloat16)
        return first, second

    def weigh(way, found):
        first, second = found
        q = q_fwd if way == 0 else q_bwd
        weight = jnp.where(first, jnp.broadcast_to(q[0:1, :], over), 0) + jnp.where(
            second, jnp.broadcast_to(q[1:2, :], over), 0)
        high = (weight >> 8).astype(jnp.float32).astype(jnp.bfloat16)
        low = (weight & 255).astype(jnp.float32).astype(jnp.bfloat16)
        for k in range(group):
            rows = pl.ds(k * cap, cap)
            hit = pick[way, rows, :]
            mix_hi[way, rows, :] = hit * jnp.broadcast_to(high[k : k + 1, :], (cap, tokens))
            mix_lo[way, rows, :] = hit * jnp.broadcast_to(low[k : k + 1, :], (cap, tokens))

    pending = []
    sources = (fwd_in, saved_in, grad_in)

    def dispatch(t, k):
        return pltpu.make_async_remote_copy(
            src_ref=packed.at[t, pl.ds(k * cap, cap)],
            dst_ref=slots.at[t, pl.ds(k * cap, cap)],
            send_sem=disp_s.at[t, k],
            recv_sem=disp_r.at[t, k],
            device_id=expert_peer(k),
            device_id_type=MESH,
        )

    def pack(t):
        way = 0 if t == 0 else 1
        rows = jnp.dot(pick[way], sources[t][0], preferred_element_type=jnp.float32)
        rows = rows.astype(jnp.bfloat16)
        slots[t, pl.ds(0, cap), :] = rows[:cap]
        packed[t, pl.ds(cap, (group - 1) * cap), :] = rows[cap:]

    def blocks(g):
        return [k for k in range(g * per_group, (g + 1) * per_group) if k > 0]

    def issue(tensors, g):
        for k in blocks(g):
            for t in tensors:
                dispatch(t, k).start()

    def drain(tensors, g):
        for k in blocks(g):
            for t in tensors:
                dispatch(t, k).wait_send()

    found_fwd = find(0)
    pack(0)
    pl.semaphore_wait(barrier, len(peers))
    queue = [(t, g) for t in ((0,), (1, 2)) for g in range(groups) if blocks(g)]
    sent = min(3, len(queue))
    for item in queue[:sent]:
        issue(*item)
    found_bwd = find(1)
    pack(1)
    pack(2)
    weigh(1, found_bwd)
    weigh(0, found_fwd)

    def part_copy(t, g, k):
        peer = lax.rem(mine + k, shards)
        return pltpu.make_async_remote_copy(
            src_ref=part_out.at[t, peer, pl.ds(g * span, span)],
            dst_ref=part_in.at[t, k - 1, pl.ds(g * span, span)],
            send_sem=part_s.at[t, g, k - 1],
            recv_sem=part_r.at[t, g, k - 1],
            device_id=shard_peer(k),
            device_id_type=MESH,
        )

    def act_copy(way, g, k):
        return pltpu.make_async_remote_copy(
            src_ref=act.at[way, mine, pl.ds(g * span, span)],
            dst_ref=act.at[way, mine, pl.ds(g * span, span)],
            send_sem=act_s.at[way, g, k - 1],
            recv_sem=act_r.at[way, g, k - 1],
            device_id=shard_peer(k),
            device_id_type=MESH,
        )

    def send_parts(t, g):
        for k in range(1, shards):
            copy = part_copy(t, g, k)
            copy.start()
            pending.append(copy)

    def arrive(t, g):
        for b in range(per_group):
            k = g * per_group + b
            if k > 0:
                dispatch(t, k).wait_recv()

    def partial(t, g):
        rows = pl.ds(g * span, span)
        arrive(t, g)

        @pl.loop(0, shards)
        def _(q):
            cols = pl.ds(pl.multiple_of(q * quarter, quarter), quarter)
            if t == 2:
                value = lax.dot_general(
                    slots[t, rows, :], w_out[cols, :], (((1,), (1,)), ((), ())),
                    preferred_element_type=jnp.float32)
            else:
                value = jnp.dot(slots[t, rows, :], w_in[:, cols],
                                preferred_element_type=jnp.float32)
            part_out[t, q, rows, :] = value.astype(jnp.bfloat16)

        send_parts(t, g)

    def total(t, g):
        rows = pl.ds(g * span, span)
        value = part_out[t, mine, rows, :].astype(jnp.float32)
        for k in range(1, shards):
            part_copy(t, g, k).wait_recv()
            value = value + part_in[t, k - 1, rows, :].astype(jnp.float32)
        return value

    def send_act(way, g, value):
        act[way, mine, pl.ds(g * span, span), :] = value.astype(jnp.bfloat16)
        for k in range(1, shards):
            copy = act_copy(way, g, k)
            copy.start()
            pending.append(copy)

    def forward_act(g):
        hidden = total(0, g)
        send_act(0, g, hidden / (1.0 + jnp.exp(-hidden)))

    def backward_act(g):
        hidden = total(1, g)
        slope = total(2, g)
        squash = 1.0 / (1.0 + jnp.exp(-hidden))
        send_act(1, g, slope * squash * (1.0 + hidden * (1.0 - squash)))

    def ret_copy(way, c, k):
        start, size = (0, features) if c is None else chunks[c]
        c = 0 if c is None else c
        view = (way, pl.ds(k * cap, cap), pl.ds(start, size))
        return pltpu.make_async_remote_copy(
            src_ref=ret_out.at[view],
            dst_ref=ret_in.at[view],
            send_sem=ret_s.at[way, c, k],
            recv_sem=ret_r.at[way, c, k],
            device_id=(sec, lax.rem(me - k + group, group), mine),
            device_id_type=MESH,
        )

    def rows_back(g):
        for k in range(1, shards):
            act_copy(1, g, k).wait_recv()
        value = None
        for q in range(shards):
            term = lax.dot_general(
                act[1, q, pl.ds(g * span, span), :], w_in[:, pl.ds(q * quarter, quarter)],
                (((1,), (1,)), ((), ())), preferred_element_type=jnp.float32)
            value = term if value is None else value + term
        value = value.astype(jnp.bfloat16)
        for b in range(per_group):
            k = g * per_group + b
            target = ret_in if k == 0 else ret_out
            target[1, pl.ds(k * cap, cap), :] = value[b * cap : (b + 1) * cap]

    def send_back(g):
        for k in blocks(g):
            copy = ret_copy(1, None, k)
            copy.start()
            pending.append(copy)

    def give_back():
        for g in range(groups):
            for k in range(1, shards):
                act_copy(0, g, k).wait_recv()
        for c, (start, size) in enumerate(chunks):
            cols = pl.ds(start, size)
            value = None
            for q in range(shards):
                term = jnp.dot(act[0, q], w_out[pl.ds(q * quarter, quarter), cols],
                               preferred_element_type=jnp.float32)
                value = term if value is None else value + term
            value = value.astype(jnp.bfloat16)
            ret_in[0, pl.ds(0, cap), cols] = value[:cap]
            ret_out[0, pl.ds(cap, (group - 1) * cap), cols] = value[cap:]

    def send_forward():
        for c in range(len(chunks)):
            for k in range(1, group):
                copy = ret_copy(0, c, k)
                copy.start()
                pending.append(copy)

    def send_last(c):
        for k in blocks(last):
            ret_copy(1, c, k).start()

    def follow(c):
        for k in blocks(last):
            ret_copy(1, c, k).wait_send()
        if c + 2 < len(chunks):
            send_last(c + 2)

    def hop_copy(way, c):
        start, size = chunks[c]
        out = fwd_out if way == 0 else bwd_out
        return pltpu.make_async_remote_copy(
            src_ref=done.at[way, :, pl.ds(start, size)],
            dst_ref=out.at[0, :, pl.ds(start, size)],
            send_sem=hop_s.at[way, c],
            recv_sem=hop_r.at[way, c],
            device_id=section_peer(1 if way == 0 else -1),
            device_id_type=MESH,
        )

    def mix(way, c):
        tok = fwd_in if way == 0 else grad_in
        across = (((0,), (0,)), ((), ()))
        start, size = chunks[c]
        cols = pl.ds(start, size)
        if way == 0:
            for k in range(1, group):
                ret_copy(0, c, k).wait_recv()
        else:
            for g in range(groups):
                for k in blocks(g):
                    if g == last:
                        ret_copy(1, c, k).wait_recv()
                    elif c == 0:
                        ret_copy(1, None, k).wait_recv()
        back = ret_in[way, :, cols]
        high = lax.dot_general(mix_hi[way], back, across, preferred_element_type=jnp.float32)
        low = lax.dot_general(mix_lo[way], back, across, preferred_element_type=jnp.float32)
        summed = (high * 256.0 + low) * (1.0 / 32768.0)
        done[way, :, cols] = (tok[0, :, cols].astype(jnp.float32) + summed).astype(jnp.bfloat16)
        copy = hop_copy(way, c)
        copy.start()
        pending.append(copy)

    load_in.wait()
    load_out.wait()
    for g in range(groups):
        partial(0, g)
        drain((0,), g)
        if blocks(g) and sent < len(queue):
            issue(*queue[sent])
            sent += 1
        if g > 0:
            forward_act(g - 1)
    for item in queue[sent:]:
        issue(*item)
    for g in range(groups):
        partial(1, g)
        partial(2, g)
        if g == 0:
            forward_act(last)
        if g < last:
            backward_act(g)
        if g == 0:
            give_back()
        elif g < last:
            rows_back(g - 1)
    for g in range(groups):
        drain((1, 2), g)
    send_forward()
    for g in range(last - 1):
        send_back(g)
    backward_act(last)
    if last > 0:
        rows_back(last - 1)
        send_back(last - 1)
    rows_back(last)
    for c in range(min(2, len(chunks))):
        send_last(c)
    for c in range(len(chunks)):
        mix(0, c)
    for c in range(len(chunks)):
        follow(c)
        mix(1, c)
    for way in (1, 0):
        for c in range(len(chunks)):
            hop_copy(way, c).wait_recv()
    for copy in pending:
        copy.wait_send()


def settle(fwd, bwd, fwd_out, bwd_out, rows, sem):
    loads = [pltpu.make_async_copy(ref, rows.at[i], sem.at[0, i])
             for i, ref in enumerate((fwd, bwd))]
    stores = [pltpu.make_async_copy(rows.at[i], ref, sem.at[1, i])
              for i, ref in enumerate((fwd_out, bwd_out))]
    for load in loads:
        load.start()
    for load, store in zip(loads, stores):
        load.wait()
        store.start()
    for store in stores:
        store.wait()


def per_device(dims_base, fwd_in, saved_in, grad_in, w_in, w_out, ids_fwd, weight_fwd, ids_bwd,
               weight_bwd):
    sections, group, shards = dims_base
    tokens, features = fwd_in.shape[1:]
    hidden = w_in.shape[3]
    assert w_in.shape[:2] == (1, 1)
    top = ids_fwd.shape[2]
    assert top == 2
    room = max(2, (tokens * top * 5 + 4 * group - 1) // (4 * group))
    cap = -(-room // ROWS) * ROWS
    groups = 4 if group % 4 == 0 else 1
    quarter = hidden // shards
    rows = group * cap
    nc = len(column_chunks(features))
    dims = (sections, group, shards, cap, tokens, features, quarter, groups)
    routing = [a[0].T for a in (ids_fwd, weight_fwd, ids_bwd, weight_bwd)]
    bf = jnp.bfloat16
    dma = pltpu.SemaphoreType.DMA
    vmem = pl.BlockSpec(memory_space=pltpu.VMEM)
    anywhere = pl.BlockSpec(memory_space=pl.ANY)
    out = jax.ShapeDtypeStruct(fwd_in.shape, bf)
    fwd, bwd = pl.pallas_call(
        functools.partial(kernel, dims),
        name="relay",
        out_shape=(out, out),
        in_specs=[vmem] * 7 + [anywhere] * 2,
        out_specs=(vmem, vmem),
        scratch_shapes=[
            pltpu.VMEM((features, hidden), bf),
            pltpu.VMEM((hidden, features), bf),
            pltpu.VMEM((2, rows, tokens), bf),
            pltpu.VMEM((2, rows, tokens), bf),
            pltpu.VMEM((2, rows, tokens), bf),
            pltpu.VMEM((3, rows, features), bf),
            pltpu.VMEM((3, rows, features), bf),
            pltpu.VMEM((3, shards, rows, quarter), bf),
            pltpu.VMEM((3, shards - 1, rows, quarter), bf),
            pltpu.VMEM((2, shards, rows, quarter), bf),
            pltpu.VMEM((2, rows, features), bf),
            pltpu.VMEM((2, rows, features), bf),
            pltpu.VMEM((2, tokens, features), bf),
            dma((2,)),
            dma((3, group)), dma((3, group)),
            dma((3, groups, shards - 1)), dma((3, groups, shards - 1)),
            dma((2, groups, shards - 1)), dma((2, groups, shards - 1)),
            dma((2, nc, group)), dma((2, nc, group)),
            dma((2, nc)), dma((2, nc)),
        ],
        compiler_params=pltpu.CompilerParams(
            collective_id=0, has_side_effects=True, vmem_limit_bytes=56 * 2**20),
    )(*routing, fwd_in, saved_in, grad_in, w_in, w_out)
    return pl.pallas_call(
        settle,
        name="settle",
        out_shape=(out, out),
        in_specs=[anywhere] * 2,
        out_specs=(anywhere, anywhere),
        scratch_shapes=[pltpu.VMEM((2,) + fwd_in.shape, bf), dma((2, 2))],
    )(fwd, bwd)


def solution(mesh):
    rows = P("section", "expert", "shard")
    slots = P("section", "expert", None)
    dims_base = (mesh.shape["section"], mesh.shape["expert"], mesh.shape["shard"])
    return jax.shard_map(
        functools.partial(per_device, dims_base),
        mesh=mesh,
        in_specs=(rows, rows, rows, P("section", "expert", "shard", None),
                  P("section", "expert", None, "shard"), slots, slots, slots, slots),
        out_specs=(rows, rows),
        check_vma=False,
    )
```

```python
import functools

import jax
import jax.numpy as jnp
from jax import lax
from jax.experimental import pallas as pl
from jax.experimental.pallas import tpu as pltpu
from jax.sharding import PartitionSpec as P

MESH = pl.DeviceIdType.MESH
LANES = 128
ROWS = 16


def column_chunks(features):
    chunks, start = [], 0
    while start < features:
        size = min(2 * LANES, features - start)
        chunks.append((start, size))
        start += size
    return chunks


def kernel(dims, ids_fwd, q_fwd, ids_bwd, q_bwd, fwd_in, saved_in, grad_in, w_in_hbm, w_out_hbm, fwd_out, bwd_out,
           w_in, w_out, pick, mix_hi, mix_lo, packed, slots, part_out, part_in, act,
           ret_out, ret_in, done, w_sem, disp_s, disp_r, part_s, part_r, act_s, act_r,
           ret_s, ret_r, hop_s, hop_r):
    sections, group, shards, cap, tokens, features, quarter, groups = dims
    per_group = group // groups
    span = per_group * cap
    chunks = column_chunks(features)
    sec = lax.axis_index("section")
    me = lax.axis_index("expert")
    mine = lax.axis_index("shard")

    load_in = pltpu.make_async_copy(w_in_hbm.at[0, 0], w_in, w_sem.at[0])
    load_out = pltpu.make_async_copy(w_out_hbm.at[0, 0], w_out, w_sem.at[1])
    load_in.start()
    load_out.start()

    def expert_peer(k):
        return (sec, lax.rem(me + k, group), mine)

    def shard_peer(k):
        return (sec, me, lax.rem(mine + k, shards))

    def section_peer(k):
        return (lax.rem(sec + k + sections, sections), me, mine)

    barrier = pltpu.get_barrier_semaphore()
    peers = [expert_peer(k) for k in range(1, group)]
    peers += [shard_peer(k) for k in range(1, shards)]
    peers += [section_peer(1), section_peer(-1)]
    for peer in peers:
        pl.semaphore_signal(barrier, inc=1, device_id=peer, device_id_type=MESH)

    upper = (lax.broadcasted_iota(jnp.int32, (tokens, tokens), 0)
             < lax.broadcasted_iota(jnp.int32, (tokens, tokens), 1)).astype(jnp.bfloat16)
    height = max(group, 8)
    labels = lax.rem(lax.broadcasted_iota(jnp.int32, (height, tokens), 0) + me, group)
    spots = lax.broadcasted_iota(jnp.int32, (cap, tokens), 0)
    over = (height, tokens)

    def find(way):
        ids = ids_fwd if way == 0 else ids_bwd
        first = jnp.broadcast_to(ids[0:1, :], over) == labels
        second = jnp.broadcast_to(ids[1:2, :], over) == labels
        named = jnp.where(first, 1, 0) + jnp.where(second, 1, 0)
        rank = jnp.dot(named.astype(jnp.float32).astype(jnp.bfloat16), upper,
                       preferred_element_type=jnp.float32).astype(jnp.int32)
        spot = jnp.where(named > 0, rank, cap)
        for k in range(group):
            hit = jnp.broadcast_to(spot[k : k + 1, :], (cap, tokens)) == spots
            pick[way, pl.ds(k * cap, cap), :] = jnp.where(hit, 1.0, 0.0).astype(jnp.bfloat16)
        return first, second

    def weigh(way, found):
        first, second = found
        q = q_fwd if way == 0 else q_bwd
        weight = jnp.where(first, jnp.broadcast_to(q[0:1, :], over), 0) + jnp.where(
            second, jnp.broadcast_to(q[1:2, :], over), 0)
        high = (weight >> 8).astype(jnp.float32).astype(jnp.bfloat16)
        low = (weight & 255).astype(jnp.float32).astype(jnp.bfloat16)
        for k in range(group):
            rows = pl.ds(k * cap, cap)
            hit = pick[way, rows, :]
            mix_hi[way, rows, :] = hit * jnp.broadcast_to(high[k : k + 1, :], (cap, tokens))
            mix_lo[way, rows, :] = hit * jnp.broadcast_to(low[k : k + 1, :], (cap, tokens))

    pending = []
    sources = (fwd_in, saved_in, grad_in)

    def dispatch(t, k):
        return pltpu.make_async_remote_copy(
            src_ref=packed.at[t, pl.ds(k * cap, cap)],
            dst_ref=slots.at[t, pl.ds(k * cap, cap)],
            send_sem=disp_s.at[t, k],
            recv_sem=disp_r.at[t, k],
            device_id=expert_peer(k),
            device_id_type=MESH,
        )

    def pack(t):
        way = 0 if t == 0 else 1
        rows = jnp.dot(pick[way], sources[t][0], preferred_element_type=jnp.float32)
        rows = rows.astype(jnp.bfloat16)
        slots[t, pl.ds(0, cap), :] = rows[:cap]
        packed[t, pl.ds(cap, (group - 1) * cap), :] = rows[cap:]

    def blocks(g):
        return [k for k in range(g * per_group, (g + 1) * per_group) if k > 0]

    def issue(tensors, g):
        for k in blocks(g):
            for t in tensors:
                dispatch(t, k).start()

    def drain(tensors, g):
        for k in blocks(g):
            for t in tensors:
                dispatch(t, k).wait_send()

    found_bwd = find(1)
    pack(1)
    pack(2)
    pl.semaphore_wait(barrier, len(peers))
    queue = [(t, g) for t in ((1, 2), (0,)) for g in range(groups) if blocks(g)]
    sent = min(3, len(queue))
    for item in queue[:sent]:
        issue(*item)
    found_fwd = find(0)
    pack(0)
    weigh(1, found_bwd)
    weigh(0, found_fwd)

    def part_copy(t, g, k):
        peer = lax.rem(mine + k, shards)
        return pltpu.make_async_remote_copy(
            src_ref=part_out.at[t, peer, pl.ds(g * span, span)],
            dst_ref=part_in.at[t, k - 1, pl.ds(g * span, span)],
            send_sem=part_s.at[t, g, k - 1],
            recv_sem=part_r.at[t, g, k - 1],
            device_id=shard_peer(k),
            device_id_type=MESH,
        )

    def act_copy(way, g, k):
        return pltpu.make_async_remote_copy(
            src_ref=act.at[way, mine, pl.ds(g * span, span)],
            dst_ref=act.at[way, mine, pl.ds(g * span, span)],
            send_sem=act_s.at[way, g, k - 1],
            recv_sem=act_r.at[way, g, k - 1],
            device_id=shard_peer(k),
            device_id_type=MESH,
        )

    def send_parts(t, g):
        for k in range(1, shards):
            copy = part_copy(t, g, k)
            copy.start()
            pending.append(copy)

    def arrive(t, g):
        for b in range(per_group):
            k = g * per_group + b
            if k > 0:
                dispatch(t, k).wait_recv()

    def partial(t, g):
        rows = pl.ds(g * span, span)
        arrive(t, g)

        @pl.loop(0, shards)
        def _(q):
            cols = pl.ds(pl.multiple_of(q * quarter, quarter), quarter)
            if t == 2:
                value = lax.dot_general(
                    slots[t, rows, :], w_out[cols, :], (((1,), (1,)), ((), ())),
                    preferred_element_type=jnp.float32)
            else:
                value = jnp.dot(slots[t, rows, :], w_in[:, cols],
                                preferred_element_type=jnp.float32)
            part_out[t, q, rows, :] = value.astype(jnp.bfloat16)

        send_parts(t, g)

    def total(t, g):
        rows = pl.ds(g * span, span)
        value = part_out[t, mine, rows, :].astype(jnp.float32)
        for k in range(1, shards):
            part_copy(t, g, k).wait_recv()
            value = value + part_in[t, k - 1, rows, :].astype(jnp.float32)
        return value

    def send_act(way, g, value):
        act[way, mine, pl.ds(g * span, span), :] = value.astype(jnp.bfloat16)
        for k in range(1, shards):
            copy = act_copy(way, g, k)
            copy.start()
            pending.append(copy)

    def forward_act(g):
        hidden = total(0, g)
        send_act(0, g, hidden / (1.0 + jnp.exp(-hidden)))

    def backward_act(g):
        hidden = total(1, g)
        slope = total(2, g)
        squash = 1.0 / (1.0 + jnp.exp(-hidden))
        send_act(1, g, slope * squash * (1.0 + hidden * (1.0 - squash)))

    def ret_copy(way, c, k):
        start, size = chunks[c] if way == 0 else (0, features)
        view = (way, pl.ds(k * cap, cap), pl.ds(start, size))
        return pltpu.make_async_remote_copy(
            src_ref=ret_out.at[view],
            dst_ref=ret_in.at[view],
            send_sem=ret_s.at[way, c, k],
            recv_sem=ret_r.at[way, c, k],
            device_id=(sec, lax.rem(me - k + group, group), mine),
            device_id_type=MESH,
        )

    def rows_back(g):
        for k in range(1, shards):
            act_copy(1, g, k).wait_recv()
        value = None
        for q in range(shards):
            term = lax.dot_general(
                act[1, q, pl.ds(g * span, span), :], w_in[:, pl.ds(q * quarter, quarter)],
                (((1,), (1,)), ((), ())), preferred_element_type=jnp.float32)
            value = term if value is None else value + term
        value = value.astype(jnp.bfloat16)
        for b in range(per_group):
            k = g * per_group + b
            target = ret_in if k == 0 else ret_out
            target[1, pl.ds(k * cap, cap), :] = value[b * cap : (b + 1) * cap]

    def send_back(g):
        for k in blocks(g):
            copy = ret_copy(1, 0, k)
            copy.start()
            pending.append(copy)

    def give_back():
        for g in range(groups):
            for k in range(1, shards):
                act_copy(0, g, k).wait_recv()
        for c, (start, size) in enumerate(chunks):
            cols = pl.ds(start, size)
            value = None
            for q in range(shards):
                term = jnp.dot(act[0, q], w_out[pl.ds(q * quarter, quarter), cols],
                               preferred_element_type=jnp.float32)
                value = term if value is None else value + term
            value = value.astype(jnp.bfloat16)
            ret_in[0, pl.ds(0, cap), cols] = value[:cap]
            ret_out[0, pl.ds(cap, (group - 1) * cap), cols] = value[cap:]
            for k in range(1, group):
                copy = ret_copy(0, c, k)
                copy.start()
                pending.append(copy)

    def hop_copy(way, c):
        start, size = chunks[c]
        out = fwd_out if way == 0 else bwd_out
        return pltpu.make_async_remote_copy(
            src_ref=done.at[way, :, pl.ds(start, size)],
            dst_ref=out.at[0, :, pl.ds(start, size)],
            send_sem=hop_s.at[way, c],
            recv_sem=hop_r.at[way, c],
            device_id=section_peer(1 if way == 0 else -1),
            device_id_type=MESH,
        )

    def mix(way, c):
        tok = fwd_in if way == 0 else grad_in
        across = (((0,), (0,)), ((), ()))
        start, size = chunks[c]
        cols = pl.ds(start, size)
        if way == 0 or c == 0:
            for k in range(1, group):
                ret_copy(way, c, k).wait_recv()
        back = ret_in[way, :, cols]
        high = lax.dot_general(mix_hi[way], back, across, preferred_element_type=jnp.float32)
        low = lax.dot_general(mix_lo[way], back, across, preferred_element_type=jnp.float32)
        summed = (high * 256.0 + low) * (1.0 / 32768.0)
        done[way, :, cols] = (tok[0, :, cols].astype(jnp.float32) + summed).astype(jnp.bfloat16)
        copy = hop_copy(way, c)
        copy.start()
        pending.append(copy)

    load_in.wait()
    load_out.wait()
    last = groups - 1
    for g in range(groups):
        partial(1, g)
        partial(2, g)
        drain((1, 2), g)
        if blocks(g) and sent < len(queue):
            issue(*queue[sent])
            sent += 1
        if g < last:
            backward_act(g)
            if g > 0:
                rows_back(g - 1)
    for item in queue[sent:]:
        issue(*item)
    partial(0, 0)
    backward_act(last)
    if last > 0:
        rows_back(last - 1)
    for g in range(groups):
        if g > 0:
            partial(0, g)
        drain((0,), g)
        if g > 0:
            send_back(g - 1)
            forward_act(g - 1)
    rows_back(last)
    send_back(last)
    forward_act(last)
    give_back()
    for c in range(len(chunks)):
        mix(1, c)
    for c in range(len(chunks)):
        mix(0, c)
    for way in (1, 0):
        for c in range(len(chunks)):
            hop_copy(way, c).wait_recv()
    for copy in pending:
        copy.wait_send()


def settle(fwd, bwd, fwd_out, bwd_out, rows, sem):
    loads = [pltpu.make_async_copy(ref, rows.at[i], sem.at[0, i])
             for i, ref in enumerate((fwd, bwd))]
    stores = [pltpu.make_async_copy(rows.at[i], ref, sem.at[1, i])
              for i, ref in enumerate((fwd_out, bwd_out))]
    for load in loads:
        load.start()
    for load, store in zip(loads, stores):
        load.wait()
        store.start()
    for store in stores:
        store.wait()


def per_device(dims_base, fwd_in, saved_in, grad_in, w_in, w_out, ids_fwd, weight_fwd, ids_bwd,
               weight_bwd):
    sections, group, shards = dims_base
    tokens, features = fwd_in.shape[1:]
    hidden = w_in.shape[3]
    assert w_in.shape[:2] == (1, 1)
    top = ids_fwd.shape[2]
    assert top == 2
    room = max(2, (tokens * top * 5 + 4 * group - 1) // (4 * group))
    cap = -(-room // ROWS) * ROWS
    groups = 4 if group % 4 == 0 else 1
    quarter = hidden // shards
    rows = group * cap
    nc = len(column_chunks(features))
    dims = (sections, group, shards, cap, tokens, features, quarter, groups)
    routing = [a[0].T for a in (ids_fwd, weight_fwd, ids_bwd, weight_bwd)]
    bf = jnp.bfloat16
    dma = pltpu.SemaphoreType.DMA
    vmem = pl.BlockSpec(memory_space=pltpu.VMEM)
    anywhere = pl.BlockSpec(memory_space=pl.ANY)
    out = jax.ShapeDtypeStruct(fwd_in.shape, bf)
    fwd, bwd = pl.pallas_call(
        functools.partial(kernel, dims),
        name="relay",
        out_shape=(out, out),
        in_specs=[vmem] * 7 + [anywhere] * 2,
        out_specs=(vmem, vmem),
        scratch_shapes=[
            pltpu.VMEM((features, hidden), bf),
            pltpu.VMEM((hidden, features), bf),
            pltpu.VMEM((2, rows, tokens), bf),
            pltpu.VMEM((2, rows, tokens), bf),
            pltpu.VMEM((2, rows, tokens), bf),
            pltpu.VMEM((3, rows, features), bf),
            pltpu.VMEM((3, rows, features), bf),
            pltpu.VMEM((3, shards, rows, quarter), bf),
            pltpu.VMEM((3, shards - 1, rows, quarter), bf),
            pltpu.VMEM((2, shards, rows, quarter), bf),
            pltpu.VMEM((2, rows, features), bf),
            pltpu.VMEM((2, rows, features), bf),
            pltpu.VMEM((2, tokens, features), bf),
            dma((2,)),
            dma((3, group)), dma((3, group)),
            dma((3, groups, shards - 1)), dma((3, groups, shards - 1)),
            dma((2, groups, shards - 1)), dma((2, groups, shards - 1)),
            dma((2, nc, group)), dma((2, nc, group)),
            dma((2, nc)), dma((2, nc)),
        ],
        compiler_params=pltpu.CompilerParams(
            collective_id=0, has_side_effects=True, vmem_limit_bytes=56 * 2**20),
    )(*routing, fwd_in, saved_in, grad_in, w_in, w_out)
    return pl.pallas_call(
        settle,
        name="settle",
        out_shape=(out, out),
        in_specs=[anywhere] * 2,
        out_specs=(anywhere, anywhere),
        scratch_shapes=[pltpu.VMEM((2,) + fwd_in.shape, bf), dma((2, 2))],
    )(fwd, bwd)


def solution(mesh):
    rows = P("section", "expert", "shard")
    slots = P("section", "expert", None)
    dims_base = (mesh.shape["section"], mesh.shape["expert"], mesh.shape["shard"])
    return jax.shard_map(
        functools.partial(per_device, dims_base),
        mesh=mesh,
        in_specs=(rows, rows, rows, P("section", "expert", "shard", None),
                  P("section", "expert", None, "shard"), slots, slots, slots, slots),
        out_specs=(rows, rows),
        check_vma=False,
    )
```
